32 devices in a mesh: layer: 2 (over y), latent: 8 (over z, x), tok: 2 (over core).
Axes of the slice: x: 2, y: 2, z: 4, core: 2. Of those that a mesh axis runs over, the one named last changes fastest.
Arguments:
- resid: bfloat16 [2, 384, 2304], P('layer', 'tok', 'latent'), may hold values from -6 to 6
- w_enc: bfloat16 [2, 2304, 2048], P('layer', None, 'latent'), may hold values from -0.09375 to 0.09375
- b_enc: float32 [2048], P('latent'), may hold values from -3 to 3
- w_dec: bfloat16 [2, 2048, 2304], P('layer', 'latent'), may hold values from -0.125 to 0.125
- b_dec: bfloat16 [2, 2304], P('layer', 'latent'), may hold values from -3 to 3
Outputs:
- grad_w_enc: bfloat16 [2, 2304, 2048], P('layer', 'tok', 'latent')
- grad_w_dec: bfloat16 [2, 2048, 2304], P('layer', 'latent')
The draws below stay inside these ranges and needn't reach their ends.
All inputs are finite; a program needn't handle non-finite values.
Results may differ from the reference program's by a relative error of at most 0.023.
Values may be sent and summed in bfloat16 or wider, within the bound.
A program may use at most 64 MiB of HBM per device.

```python
import jax
import jax.numpy as jnp
from jax import lax

D = 2304
H_DEV = 256
TOK_DEV = 192
H = 2048
LAYERS = 2
TOKENS = 384
N_LATENT = 8
N_TOK = 2


def block_levels(rng, dims, shards, least, high):
    factor_of, own = 1.0, jax.random.fold_in(rng, 6)
    for axis_at, blocks in shards:
        steps = jnp.exp(jax.random.uniform(jax.random.fold_in(own, axis_at), (blocks,), jnp.float32, least / len(shards), high / len(shards)))
        factor_of = factor_of * jnp.repeat(steps, dims[axis_at] // blocks).reshape([-1 if axis == axis_at else 1 for axis in range(len(dims))])
    return factor_of


def noise(stream_key, extent, deviation, reach, cuts=(), dtype=jnp.bfloat16):
    drawn = deviation * jax.random.normal(stream_key, extent, jnp.float32)
    if cuts:
        drawn = drawn * block_levels(stream_key, extent, cuts, -0.22, 0.18)
    return jnp.clip(drawn, -reach, reach).astype(dtype)


def setup_inputs(seed: int = 0) -> dict:
    key_list = jax.random.split(jax.random.key(seed), 6)
    return {
        "resid": noise(key_list[0], (LAYERS, TOKENS, D), 1.0, 6.0, ((0, 2), (1, 2), (2, 8))),
        "w_enc": noise(key_list[1], (LAYERS, D, H), (D * LAYERS) ** -0.5, 0.09375, ((0, 2), (2, 8))),
        "b_enc": noise(key_list[2], (H,), 0.5, 3.0, ((0, 8),), jnp.float32),
        "w_dec": noise(key_list[3], (LAYERS, H, D), H ** -0.5, 0.125, ((0, 2), (1, 8))),
        "b_dec": noise(key_list[4], (LAYERS, D), 0.5, 3.0, ((0, 2), (1, 8))),
    }


BETA = 4.0


def halves(left, right):
    total = jnp.zeros((left.shape[1], right.shape[1]), jnp.float32)
    for block in range(N_TOK):
        lo = block * TOK_DEV
        part = jnp.dot(left[lo:lo + TOK_DEV].T, right[lo:lo + TOK_DEV], preferred_element_type=jnp.float32)
        part = lax.optimization_barrier(part.astype(jnp.bfloat16)).astype(jnp.float32)
        total = total + part
    return total.astype(jnp.bfloat16)


def slab_sum(act, layer_w):
    act_slabs = jnp.transpose(act.reshape(TOKENS, N_LATENT, H_DEV), (1, 0, 2))
    w_slabs = layer_w.reshape(N_LATENT, H_DEV, D)

    def add_slab(carry, items):
        act_slab, w_slab = items
        part = jnp.dot(act_slab, w_slab, preferred_element_type=jnp.float32)
        part = lax.optimization_barrier(part.astype(jnp.bfloat16)).astype(jnp.float32)
        return carry + part, None

    total, _ = lax.scan(add_slab, jnp.zeros((TOKENS, D), jnp.float32), (act_slabs, w_slabs))
    return total


def reference(resid, w_enc, b_enc, w_dec, b_dec):
    def encode(carry, items):
        layer_x, layer_w = items
        return carry + jnp.dot(layer_x, layer_w, preferred_element_type=jnp.float32), None

    start = jnp.broadcast_to(b_enc.astype(jnp.float32), (TOKENS, H))
    pre, _ = lax.scan(encode, start, (resid, w_enc))
    act = (jax.nn.softplus(BETA * pre) / BETA).astype(jnp.bfloat16)
    slope = jax.nn.sigmoid(BETA * pre)

    def decode(carry, items):
        layer_x, layer_w, layer_b = items
        recon = slab_sum(act, layer_w) + layer_b.astype(jnp.float32)
        grad_recon = ((2.0 / TOKENS) * (recon - layer_x.astype(jnp.float32))).astype(jnp.bfloat16)
        carry = carry + jnp.dot(grad_recon, layer_w.T, preferred_element_type=jnp.float32)
        return carry, halves(act, grad_recon)

    grad_act, grad_w_dec = lax.scan(decode, jnp.zeros((TOKENS, H), jnp.float32), (resid, w_dec, b_dec))
    grad_pre = (grad_act * slope).astype(jnp.bfloat16)
    grad_w_enc = lax.map(lambda layer_x: halves(layer_x, grad_pre), resid)
    return grad_w_enc, grad_w_dec
```

```python
import functools

import jax
import jax.numpy as jnp
from jax import lax
from jax.experimental import pallas as pl
from jax.experimental.pallas import tpu as pltpu
from jax.sharding import PartitionSpec as P

BETA = 4.0
LANES = 128
MESH = pl.DeviceIdType.MESH
F32 = jnp.float32
BF16 = jnp.bfloat16


def plain_shards(resid, w_enc, b_enc, w_dec, b_dec):
    decoder = w_dec[0]
    x_full = lax.all_gather(resid, "latent", axis=2, tiled=True)[0]
    bias_full = lax.all_gather(b_dec.reshape(1, 1, -1), "latent", axis=2, tiled=True)
    bias_full = bias_full.reshape(-1).astype(F32)
    tokens = x_full.shape[0] * lax.axis_size("tok")
    partial_value = jnp.dot(x_full, w_enc[0], preferred_element_type=F32)
    pre = lax.psum(partial_value.astype(BF16), "layer").astype(F32) + b_enc
    act = (jax.nn.softplus(BETA * pre) / BETA).astype(BF16)
    slope = jax.nn.sigmoid(BETA * pre)
    recon = lax.psum(
        jnp.dot(act, decoder, preferred_element_type=F32).astype(BF16), "latent"
    ).astype(F32)
    grad_all = (2.0 / tokens * (recon + bias_full - x_full.astype(F32))).astype(BF16)
    dec_sum = lax.dot_general(
        act, grad_all, (((0,), (0,)), ((), ())), preferred_element_type=F32
    )
    act_grad = lax.dot_general(
        grad_all, decoder, (((1,), (1,)), ((), ())), preferred_element_type=F32
    )
    grad_act = lax.psum(act_grad.astype(BF16), "layer").astype(F32)
    grad_pre = (grad_act * slope).astype(BF16)
    grad_w_dec = lax.psum(dec_sum.astype(BF16), "tok")
    grad_w_enc = lax.psum_scatter(
        lax.dot_general(
            x_full, grad_pre, (((0,), (0,)), ((), ())), preferred_element_type=F32
        ).astype(BF16),
        "tok",
        scatter_dimension=0,
        tiled=True,
    )
    return (grad_w_enc[None], grad_w_dec[None])


def kernel(
    n_lat, tokens,
    x_ref, we_hbm, be_ref, wd_hbm, bd_ref,
    oe_ref, od_ref,
    we, wdv, wd, xb, xo, xt, gb, go, pre, slope, act, act_t, act_o, ys, yr, hs, hr, gp, gp_o,
    xs, xr, zs, zr,
    load_sem, x_ss, x_rs, xo_rs, g_ss, g_rs, go_rs, one_ss, one_rs, xs_ss, xr_rs, zs_ss, zr_rs,
):
    rows, feats = x_ref.shape
    hid = we.shape[1]
    main = feats // LANES * LANES
    tiles = main // LANES
    rest = feats - main
    groups = LANES // rest
    sub = rows // groups
    nz = n_lat // 2
    half = n_lat // 2

    lay = lax.axis_index("layer")
    lat = lax.axis_index("latent")
    tok = lax.axis_index("tok")
    z, xx = lat // 2, lat % 2
    across = 2 * z + 1 - xx
    lay_o, tok_o = 1 - lay, 1 - tok

    we_load = pltpu.make_async_copy(we_hbm, we, load_sem.at[0])
    wd_load = pltpu.make_async_copy(wd_hbm, wdv, load_sem.at[1])
    we_load.start()
    wd_load.start()

    barrier = pltpu.get_barrier_semaphore()
    for d in range(1, nz):
        pl.semaphore_signal(
            barrier, inc=1, device_id={"latent": 2 * ((z + d) % nz) + xx}, device_id_type=MESH
        )
    pl.semaphore_signal(barrier, inc=1, device_id={"latent": across}, device_id_type=MESH)
    pl.semaphore_signal(barrier, inc=1, device_id={"layer": lay_o}, device_id_type=MESH)
    pl.semaphore_signal(barrier, inc=1, device_id={"tok": tok_o}, device_id_type=MESH)

    def remote(src, dst, ss, rs, where):
        return pltpu.make_async_remote_copy(
            src_ref=src, dst_ref=dst, send_sem=ss, recv_sem=rs,
            device_id=where, device_id_type=MESH,
        )

    lane = lax.broadcasted_iota(jnp.int32, (sub, LANES), 1) // rest

    def pack(full):
        out = jnp.zeros((sub, LANES), F32)
        for g in range(groups):
            out = jnp.where(lane == g, full[g * sub:(g + 1) * sub, main:], out)
        return jnp.concatenate(
            [full[:, i * LANES:(i + 1) * LANES] for i in range(tiles)] + [out], axis=0
        )

    def spread(block):
        packed = block[tiles * rows:]
        zero = jnp.zeros_like(packed)
        parts = jnp.concatenate(
            [jnp.where(lane == g, packed, zero) for g in range(groups)], axis=0
        )
        return jnp.concatenate(
            [block[i * rows:(i + 1) * rows] for i in range(tiles)] + [parts], axis=1
        )

    def gather(buf, ss, rs, use, to_tok):
        def up(j):
            return remote(buf.at[j], buf.at[j], ss.at[0, j], rs.at[j], {"latent": lat + 2})

        def down(j):
            return remote(buf.at[j], buf.at[j], ss.at[1, j], rs.at[j], {"latent": lat - 2})

        def side(j):
            return remote(buf.at[j], buf.at[j], ss.at[2, j], rs.at[j], {"latent": across})

        @pl.when(z < nz - 1)
        def _():
            up(lat).start()

        @pl.when(z > 0)
        def _():
            down(lat).start()

        side(lat).start()
        to_tok(lat)
        use(lat)

        def far(s):
            @pl.when(z - s >= 0)
            def _():
                j = across - 2 * s
                side(j).wait_recv()
                to_tok(j)
                use(j)

            @pl.when(z + s < nz)
            def _():
                j = across + 2 * s
                side(j).wait_recv()
                to_tok(j)
                use(j)

        for s in range(1, nz):
            @pl.when(z - s >= 0)
            def _():
                j = lat - 2 * s
                side(j).wait_recv()

                @pl.when(z < nz - 1)
                def _():
                    up(j).start()

                side(j).start()
                to_tok(j)
                use(j)

            @pl.when(z + s < nz)
            def _():
                j = lat + 2 * s
                side(j).wait_recv()

                @pl.when(z > 0)
                def _():
                    down(j).start()

                side(j).start()
                to_tok(j)
                use(j)

            if s == 1:
                side(across).wait_recv()
                to_tok(across)
                use(across)
            else:
                far(s - 1)
        far(nz - 1)

        def finish():
            side(lat).wait_send()

            @pl.when(z < nz - 1)
            def _():
                up(lat).wait_send()

            @pl.when(z > 0)
            def _():
                down(lat).wait_send()

            for s in range(1, nz):
                @pl.when(z - s >= 0)
                def _():
                    j = lat - 2 * s
                    side(j).wait_send()

                    @pl.when(z < nz - 1)
                    def _():
                        up(j).wait_send()

                @pl.when(z + s < nz)
                def _():
                    j = lat + 2 * s
                    side(j).wait_send()

                    @pl.when(z > 0)
                    def _():
                        down(j).wait_send()

        return finish

    tail = x_ref[:, main:]
    wide = jnp.concatenate([x_ref[:, :main]] + [tail] * groups, axis=1)
    xb[lat] = pack(wide.astype(F32)).astype(BF16)
    pre[...] = jnp.zeros_like(pre)

    pl.semaphore_wait(barrier, nz + 2)

    def x_tok(i):
        return remote(
            xb.at[half * tok_o + i], xo.at[i], x_ss.at[3, i], xo_rs.at[i], {"tok": tok_o}
        )

    def x_to_tok(j):
        @pl.when(j // half == tok_o)
        def _():
            x_tok(j - half * tok_o).start()

    def encode(j):
        lo = pl.multiple_of(j * feats, rest)
        w_main = we[pl.ds(lo, main), :]
        w_rest = we[pl.ds(pl.multiple_of(lo + main, rest), rest), :]
        w = jnp.concatenate([w_main] + [w_rest] * groups, axis=0)
        pre[...] += jnp.dot(spread(xb[j]), w, preferred_element_type=F32)

    first = []

    def encode_first(j):
        if not first:
            first.append(1)
            we_load.wait()
            encode(j)
            wd_load.wait()
            for k in range(n_lat):
                lo = k * feats
                w_rest = wdv[:, lo + main:lo + feats]
                wd[k] = jnp.concatenate([wdv[:, lo:lo + main]] + [w_rest] * groups, axis=1)
        else:
            encode(j)

    x_done = gather(xb, x_ss, x_rs, encode_first, x_to_tok)

    ys[...] = pre[...].astype(BF16)
    y_copy = remote(ys, yr, one_ss.at[0], one_rs.at[0], {"layer": lay_o})
    y_copy.start()
    y_copy.wait_recv()
    v = BETA * (pre[...] + yr[...].astype(F32) + be_ref[...])
    e = jnp.exp(-jnp.abs(v))
    act[...] = ((jnp.maximum(v, 0.0) + jnp.log1p(e)) / BETA).astype(BF16)
    slope[...] = jnp.where(v >= 0, 1.0, e) / (1.0 + e)

    def other(k):
        hi = z // (nz // 2)
        m = z + hi * (nz - 1 - 2 * z)
        if k == nz - 1:
            return z
        vv = nz - 1 - k - (m + k) // (nz - 1)
        return vv + hi * (nz - 1 - 2 * vv)

    def x_send(zt):
        return remote(xs.at[zt], xr.at[zt], xs_ss.at[zt], xr_rs.at[zt], {"latent": across})

    def z_send(zt):
        return remote(zs.at[zt], zr.at[z], zs_ss.at[zt], zr_rs.at[z], {"latent": 2 * zt + xx})

    def z_recv(zt):
        return remote(zs.at[zt], zr.at[zt], zs_ss.at[zt], zr_rs.at[zt], {"latent": 2 * zt + xx})

    def decode(j):
        return pack(jnp.dot(act[...], wd[j], preferred_element_type=F32))

    for k in range(nz):
        zt = other(k)
        xs[zt] = decode(2 * zt + 1 - xx).astype(BF16)
        x_send(zt).start()
    a_copy = remote(act, act_o, one_ss.at[1], one_rs.at[1], {"tok": tok_o})
    a_copy.start()
    for k in range(nz - 1):
        zt = other(k)
        mine = decode(2 * zt + xx)
        x_send(zt).wait_recv()
        zs[zt] = (mine + xr[zt].astype(F32)).astype(BF16)
        z_send(zt).start()
    total = decode(lat)
    bias = bd_ref[...].astype(F32)
    bias = jnp.concatenate([bias[:, :main]] + [bias[:, main:]] * groups, axis=1)
    total += jnp.concatenate(
        [jnp.broadcast_to(bias[:, i * LANES:(i + 1) * LANES], (rows, LANES)) for i in range(tiles)]
        + [jnp.broadcast_to(bias[:, main:], (sub, LANES))],
        axis=0,
    ) - xb[lat].astype(F32)
    for i in range(half):
        x_tok(i).wait_recv()
        both = jnp.concatenate([spread(xb[half * tok + i]), spread(xo[i])], axis=0)
        xt[i] = both.T
    a_copy.wait_recv()
    act_t[...] = jnp.concatenate([act[...], act_o[...]], axis=0).T
    x_send(z).wait_recv()
    total += xr[z].astype(F32)
    for k in reversed(range(nz - 1)):
        zt = other(k)
        z_recv(zt).wait_recv()
        total += zr[zt].astype(F32)
    gb[lat] = (2.0 / tokens * total).astype(BF16)
    pre[...] = jnp.zeros_like(pre)

    def g_tok(j):
        return remote(gb.at[j], go.at[j], g_ss.at[3, j], go_rs.at[j], {"tok": tok_o})

    def g_to_tok(j):
        g_tok(j).start()

    def back(j):
        pre[...] += lax.dot_general(
            spread(gb[j]), wd[j], (((1,), (1,)), ((), ())), preferred_element_type=F32
        )

    g_done = gather(gb, g_ss, g_rs, back, g_to_tok)

    hs[...] = pre[...].astype(BF16)
    h_copy = remote(hs, hr, one_ss.at[2], one_rs.at[2], {"layer": lay_o})
    h_copy.start()

    row = []
    for j in range(n_lat):
        g_tok(j).wait_recv()
        both = jnp.concatenate([spread(gb[j]), spread(go[j])], axis=0)
        dw = jnp.dot(act_t[...], both, preferred_element_type=F32)
        r = dw[:, main:main + rest]
        for g in range(1, groups):
            r = r + dw[:, main + g * rest:main + (g + 1) * rest]
        row += [dw[:, :main], r]
        if (j + 1) * feats % LANES == 0:
            width = sum(p.shape[1] for p in row)
            od_ref[:, (j + 1) * feats - width:(j + 1) * feats] = jnp.concatenate(
                row, axis=1
            ).astype(BF16)
            row = []

    h_copy.wait_recv()
    gp[...] = ((pre[...] + hr[...].astype(F32)) * slope[...]).astype(BF16)
    p_copy = remote(gp, gp_o, one_ss.at[3], one_rs.at[3], {"tok": tok_o})
    p_copy.start()
    p_copy.wait_recv()
    gp_both = jnp.concatenate([gp[...], gp_o[...]], axis=0)
    for i in range(half):
        dw = jnp.dot(xt[i], gp_both, preferred_element_type=F32)
        r = dw[main:main + rest]
        for g in range(1, groups):
            r = r + dw[main + g * rest:main + (g + 1) * rest]
        oe_ref[i * feats:(i + 1) * feats] = jnp.concatenate([dw[:main], r], axis=0).astype(BF16)

    x_done()
    g_done()
    for i in range(half):
        x_tok(i).wait_send()
    for j in range(n_lat):
        g_tok(j).wait_send()
    y_copy.wait_send()
    a_copy.wait_send()
    h_copy.wait_send()
    p_copy.wait_send()
    for k in range(nz):
        x_send(other(k)).wait_send()
    for k in range(nz - 1):
        z_send(other(k)).wait_send()


def fused_shards(n_lat, resid, w_enc, b_enc, w_dec, b_dec):
    x, we, wd = resid[0], w_enc[0], w_dec[0]
    rows, feats = x.shape
    total, hid = we.shape
    main = feats // LANES * LANES
    wide = main + LANES
    block = rows * feats // LANES
    half, nz = n_lat // 2, n_lat // 2
    dma = pltpu.SemaphoreType.DMA
    vm = pltpu.VMEM
    blocks = vm((n_lat, block, LANES), BF16)
    blocks_z = vm((nz, block, LANES), BF16)
    square = vm((rows, hid), BF16)
    in_vmem = pl.BlockSpec(memory_space=pltpu.VMEM)
    anywhere = pl.BlockSpec(memory_space=pl.ANY)
    ge, gd = pl.pallas_call(
        functools.partial(kernel, n_lat, rows * 2),
        out_shape=(
            jax.ShapeDtypeStruct((half * feats, hid), BF16),
            jax.ShapeDtypeStruct((hid, total), BF16),
        ),
        in_specs=[in_vmem, anywhere, in_vmem, anywhere, in_vmem],
        out_specs=(in_vmem, in_vmem),
        scratch_shapes=[
            vm((total, hid), BF16),
            vm((hid, total), BF16),
            vm((n_lat, hid, wide), BF16),
            blocks,
            vm((half, block, LANES), BF16),
            vm((half, wide, 2 * rows), BF16),
            blocks, blocks,
            vm((rows, hid), F32), vm((rows, hid), F32),
            square, vm((hid, 2 * rows), BF16), square,
            square, square, square, square, square, square,
            blocks_z, blocks_z, blocks_z, blocks_z,
            dma((2,)),
            dma((4, n_lat)), dma((n_lat,)), dma((half,)),
            dma((4, n_lat)), dma((n_lat,)), dma((n_lat,)),
            dma((4,)), dma((4,)),
            dma((nz,)), dma((nz,)), dma((nz,)), dma((nz,)),
        ],
        compiler_params=pltpu.CompilerParams(
            collective_id=0, has_side_effects=True, vmem_limit_bytes=48 * 2**20
        ),
    )(x, we, b_enc.reshape(1, -1), wd, b_dec)
    return ge[None], gd[None]


def packs(mesh, rows, feats):
    rest = feats % LANES
    if mesh.shape["layer"] != 2 or mesh.shape["tok"] != 2 or mesh.shape["latent"] % 4:
        return False
    if rest == 0 or rest % 32 or LANES % rest:
        return False
    return rows % (16 * (LANES // rest)) == 0 and feats > LANES


def solution(mesh):
    def shards(resid, w_enc, b_enc, w_dec, b_dec):
        _, rows, feats = resid.shape
        if packs(mesh, rows, feats) and resid.shape[0] == 1:
            return fused_shards(mesh.shape["latent"], resid, w_enc, b_enc, w_dec, b_dec)
        return plain_shards(resid, w_enc, b_enc, w_dec, b_dec)

    placed = (
        P("layer", "tok", "latent"),
        P("layer", None, "latent"),
        P("latent"),
        P("layer", "latent", None),
        P("layer", "latent"),
    )
    return jax.shard_map(
        shards,
        mesh=mesh,
        in_specs=placed,
        out_specs=(P("layer", "tok", "latent"), P("layer", "latent", None)),
        check_vma=False,
    )
```

```python
import functools

import jax
import jax.numpy as jnp
from jax import lax
from jax.experimental import pallas as pl
from jax.experimental.pallas import tpu as pltpu
from jax.sharding import PartitionSpec as P

BETA = 4.0
LANES = 128
CHUNKS = 3
MESH = pl.DeviceIdType.MESH
F32 = jnp.float32
BF16 = jnp.bfloat16


def plain_shards(resid, w_enc, b_enc, w_dec, b_dec):
    decoder = w_dec[0]
    x_full = lax.all_gather(resid, "latent", axis=2, tiled=True)[0]
    bias_full = lax.all_gather(b_dec.reshape(1, 1, -1), "latent", axis=2, tiled=True)
    bias_full = bias_full.reshape(-1).astype(F32)
    tokens = x_full.shape[0] * lax.axis_size("tok")
    partial_value = jnp.dot(x_full, w_enc[0], preferred_element_type=F32)
    pre = lax.psum(partial_value.astype(BF16), "layer").astype(F32) + b_enc
    act = (jax.nn.softplus(BETA * pre) / BETA).astype(BF16)
    slope = jax.nn.sigmoid(BETA * pre)
    recon = lax.psum(
        jnp.dot(act, decoder, preferred_element_type=F32).astype(BF16), "latent"
    ).astype(F32)
    grad_all = (2.0 / tokens * (recon + bias_full - x_full.astype(F32))).astype(BF16)
    dec_sum = lax.dot_general(
        act, grad_all, (((0,), (0,)), ((), ())), preferred_element_type=F32
    )
    act_grad = lax.dot_general(
        grad_all, decoder, (((1,), (1,)), ((), ())), preferred_element_type=F32
    )
    grad_act = lax.psum(act_grad.astype(BF16), "layer").astype(F32)
    grad_pre = (grad_act * slope).astype(BF16)
    grad_w_dec = lax.psum(dec_sum.astype(BF16), "tok")
    grad_w_enc = lax.psum_scatter(
        lax.dot_general(
            x_full, grad_pre, (((0,), (0,)), ((), ())), preferred_element_type=F32
        ).astype(BF16),
        "tok",
        scatter_dimension=0,
        tiled=True,
    )
    return (grad_w_enc[None], grad_w_dec[None])


def kernel(
    n_lat, tokens,
    x_hbm, we_hbm, be_hbm, wd_hbm, bd_hbm,
    oe_ref, od_ref,
    x_ref, be_ref, bd_ref, we, wdv, wd, xb, xo, xt, gb, go, pre, slope, act, act_t, act_o, ys, yr, hs, hr, gp, gp_o,
    xs, xr, zs, cr, mine,
    load_sem, x_ss, x_rs, xo_rs, g_ss, g_rs, go_rs, one_ss, one_rs, xs_ss, xr_rs, zs_ss, cr_rs,
):
    rows, feats = x_ref.shape
    hid = we.shape[1]
    main = feats // LANES * LANES
    tiles = main // LANES
    rest = feats - main
    groups = LANES // rest
    sub = rows // groups
    nz = n_lat // 2
    half = n_lat // 2

    lay = lax.axis_index("layer")
    lat = lax.axis_index("latent")
    tok = lax.axis_index("tok")
    z, xx = lat // 2, lat % 2
    across = 2 * z + 1 - xx
    lay_o, tok_o = 1 - lay, 1 - tok

    loads = [
        pltpu.make_async_copy(src, dst, load_sem.at[i])
        for i, (src, dst) in enumerate(
            [(x_hbm, x_ref), (we_hbm, we), (wd_hbm, wdv), (be_hbm, be_ref), (bd_hbm, bd_ref)]
        )
    ]
    for load in loads:
        load.start()
    x_load, we_load, wd_load, be_load, bd_load = loads

    barrier = pltpu.get_barrier_semaphore()

    def greet(where):
        pl.semaphore_signal(barrier, inc=1, device_id=where, device_id_type=MESH)

    greet({"latent": across})
    greet({"layer": lay_o})
    greet({"tok": tok_o})

    @pl.when(z < nz - 1)
    def _():
        greet({"latent": lat + 2})

    @pl.when(z > 0)
    def _():
        greet({"latent": lat - 2})

    def remote(src, dst, ss, rs, where):
        return pltpu.make_async_remote_copy(
            src_ref=src, dst_ref=dst, send_sem=ss, recv_sem=rs,
            device_id=where, device_id_type=MESH,
        )

    lane = lax.broadcasted_iota(jnp.int32, (sub, LANES), 1) // rest

    def pack(full):
        out = jnp.zeros((sub, LANES), F32)
        for g in range(groups):
            out = jnp.where(lane == g, full[g * sub:(g + 1) * sub, main:], out)
        return jnp.concatenate(
            [full[:, i * LANES:(i + 1) * LANES] for i in range(tiles)] + [out], axis=0
        )

    def spread(block):
        packed = block[tiles * rows:]
        zero = jnp.zeros_like(packed)
        parts = jnp.concatenate(
            [jnp.where(lane == g, packed, zero) for g in range(groups)], axis=0
        )
        return jnp.concatenate(
            [block[i * rows:(i + 1) * rows] for i in range(tiles)] + [parts], axis=1
        )

    size = xb.shape[1]
    chunk = size // CHUNKS

    def part(ref, *at, c):
        return ref.at[(*at, pl.ds(c * chunk, chunk))]

    def if_up(fn):
        pl.when(z < nz - 1)(fn)

    def if_down(fn):
        pl.when(z > 0)(fn)

    def gather(buf, ss, rs, use, to_tok):
        def send(way, j, c):
            where = {"latent": (lat + 2, lat - 2, across)[way]}
            return remote(
                part(buf, j, c=c), part(buf, j, c=c), ss.at[way, j, c], rs.at[j, c], where
            )

        for c in range(CHUNKS):
            if_up(lambda: send(0, lat, c).start())
            if_down(lambda: send(1, lat, c).start())
            send(2, lat, c).start()
        to_tok(lat)
        use(lat)

        def side_block(j):
            for c in range(CHUNKS):
                send(2, j, c).wait_recv()
            to_tok(j)
            use(j)

        def far(s):
            pl.when(z - s >= 0)(lambda: side_block(across - 2 * s))
            pl.when(z + s < nz)(lambda: side_block(across + 2 * s))

        for s in range(1, nz):
            for c in range(CHUNKS):
                @pl.when(z - s >= 0)
                def _():
                    j = lat - 2 * s
                    send(2, j, c).wait_recv()
                    if_up(lambda: send(0, j, c).start())
                    send(2, j, c).start()

                @pl.when(z + s < nz)
                def _():
                    j = lat + 2 * s
                    send(2, j, c).wait_recv()
                    if_down(lambda: send(1, j, c).start())
                    send(2, j, c).start()

            @pl.when(z - s >= 0)
            def _():
                to_tok(lat - 2 * s)
                use(lat - 2 * s)

            @pl.when(z + s < nz)
            def _():
                to_tok(lat + 2 * s)
                use(lat + 2 * s)

            if s == 1:
                side_block(across)
            else:
                far(s - 1)
        far(nz - 1)

        def finish():
            for c in range(CHUNKS):
                send(2, lat, c).wait_send()
                if_up(lambda: send(0, lat, c).wait_send())
                if_down(lambda: send(1, lat, c).wait_send())
                for s in range(1, nz):
                    @pl.when(z - s >= 0)
                    def _():
                        send(2, lat - 2 * s, c).wait_send()
                        if_up(lambda: send(0, lat - 2 * s, c).wait_send())

                    @pl.when(z + s < nz)
                    def _():
                        send(2, lat + 2 * s, c).wait_send()
                        if_down(lambda: send(1, lat + 2 * s, c).wait_send())

        return finish

    x_load.wait()
    tail = x_ref[:, main:]
    wide = jnp.concatenate([x_ref[:, :main]] + [tail] * groups, axis=1)
    xb[lat] = pack(wide.astype(F32)).astype(BF16)
    pre[...] = jnp.zeros_like(pre)

    pl.semaphore_wait(barrier, 3 + (z + nz - 1) // nz + (2 * nz - 2 - z) // nz)

    def x_tok(i):
        return remote(
            xb.at[half * tok_o + i], xo.at[i], x_ss.at[3, i, 0], xo_rs.at[i], {"tok": tok_o}
        )

    def x_to_tok(j):
        @pl.when(j // half == tok_o)
        def _():
            x_tok(j - half * tok_o).start()

    def encode(j):
        lo = pl.multiple_of(j * feats, rest)
        w_main = we[pl.ds(lo, main), :]
        w_rest = we[pl.ds(pl.multiple_of(lo + main, rest), rest), :]
        w = jnp.concatenate([w_main] + [w_rest] * groups, axis=0)
        pre[...] += jnp.dot(spread(xb[j]), w, preferred_element_type=F32)

    first = []

    def encode_first(j):
        if not first:
            first.append(1)
            we_load.wait()
            encode(j)
            wd_load.wait()
            for k in range(n_lat):
                lo = k * feats
                w_rest = wdv[:, lo + main:lo + feats]
                wd[k] = jnp.concatenate([wdv[:, lo:lo + main]] + [w_rest] * groups, axis=1)
        else:
            encode(j)

    x_done = gather(xb, x_ss, x_rs, encode_first, x_to_tok)

    ys[...] = pre[...].astype(BF16)
    y_copy = remote(ys, yr, one_ss.at[0], one_rs.at[0], {"layer": lay_o})
    y_copy.start()
    be_load.wait()
    bd_load.wait()
    y_copy.wait_recv()
    v = BETA * (pre[...] + yr[...].astype(F32) + be_ref[...])
    e = jnp.exp(-jnp.abs(v))
    act[...] = ((jnp.maximum(v, 0.0) + jnp.log1p(e)) / BETA).astype(BF16)
    slope[...] = jnp.where(v >= 0, 1.0, e) / (1.0 + e)

    order = [sign * d for d in range(nz - 1, 0, -1) for sign in (1, -1)]

    def each(fn):
        for d in order:
            pl.when(jnp.logical_and(z + d >= 0, z + d < nz))(functools.partial(fn, d))

    def x_send(zt, c):
        return remote(
            part(xs, zt, c=c), part(xr, zt, c=c), xs_ss.at[zt, c], xr_rs.at[zt, c],
            {"latent": across},
        )

    def z_send(way, zt, c):
        where = {"latent": (lat + 2, lat - 2)[way]}
        return remote(
            part(zs, zt, c=c), part(cr, way, zt, c=c), zs_ss.at[zt, c], cr_rs.at[way, zt, c], where
        )

    def decode(j):
        return pack(jnp.dot(act[...], wd[j], preferred_element_type=F32))

    def x_out(d):
        zt = z + d
        xs[zt] = decode(2 * zt + 1 - xx).astype(BF16)
        for c in range(CHUNKS):
            x_send(zt, c).start()

    def z_out(d):
        zt, way = z + d, (0 if d > 0 else 1)
        mine[...] = decode(2 * zt + xx)
        for c in range(CHUNKS):
            lo = pl.ds(c * chunk, chunk)
            x_send(zt, c).wait_recv()
            mine[lo] += xr[zt, lo].astype(F32)

            @pl.when(z > 0 if d > 0 else z < nz - 1)
            def _():
                z_send(way, zt, c).wait_recv()
                mine[lo] += cr[way, zt, lo].astype(F32)

            zs[zt, lo] = mine[lo].astype(BF16)
            z_send(way, zt, c).start()

    each(x_out)
    x_out(0)
    a_copy = remote(act, act_o, one_ss.at[1], one_rs.at[1], {"tok": tok_o})
    a_copy.start()
    each(z_out)
    total = decode(lat)
    bias = bd_ref[...].astype(F32)
    bias = jnp.concatenate([bias[:, :main]] + [bias[:, main:]] * groups, axis=1)
    total += jnp.concatenate(
        [jnp.broadcast_to(bias[:, i * LANES:(i + 1) * LANES], (rows, LANES)) for i in range(tiles)]
        + [jnp.broadcast_to(bias[:, main:], (sub, LANES))],
        axis=0,
    ) - xb[lat].astype(F32)
    for i in range(half):
        x_tok(i).wait_recv()
        both = jnp.concatenate([spread(xb[half * tok + i]), spread(xo[i])], axis=0)
        xt[i] = both.T
    a_copy.wait_recv()
    act_t[...] = jnp.concatenate([act[...], act_o[...]], axis=0).T
    mine[...] = total
    for c in range(CHUNKS):
        x_send(z, c).wait_recv()
    mine[...] += xr[z].astype(F32)

    def last(way):
        for c in range(CHUNKS):
            z_send(way, z, c).wait_recv()
        mine[...] += cr[way, z].astype(F32)

    if_down(lambda: last(0))
    if_up(lambda: last(1))
    total = mine[...]
    gb[lat] = (2.0 / tokens * total).astype(BF16)
    pre[...] = jnp.zeros_like(pre)

    def g_tok(j):
        return remote(gb.at[j], go.at[j], g_ss.at[3, j, 0], go_rs.at[j], {"tok": tok_o})

    def g_to_tok(j):
        g_tok(j).start()

    def back(j):
        pre[...] += lax.dot_general(
            spread(gb[j]), wd[j], (((1,), (1,)), ((), ())), preferred_element_type=F32
        )

    g_done = gather(gb, g_ss, g_rs, back, g_to_tok)

    hs[...] = pre[...].astype(BF16)
    h_copy = remote(hs, hr, one_ss.at[2], one_rs.at[2], {"layer": lay_o})
    h_copy.start()

    row = []
    for j in range(n_lat):
        g_tok(j).wait_recv()
        both = jnp.concatenate([spread(gb[j]), spread(go[j])], axis=0)
        dw = jnp.dot(act_t[...], both, preferred_element_type=F32)
        r = dw[:, main:main + rest]
        for g in range(1, groups):
            r = r + dw[:, main + g * rest:main + (g + 1) * rest]
        row += [dw[:, :main], r]
        if (j + 1) * feats % LANES == 0:
            width = sum(p.shape[1] for p in row)
            od_ref[:, (j + 1) * feats - width:(j + 1) * feats] = jnp.concatenate(
                row, axis=1
            ).astype(BF16)
            row = []

    h_copy.wait_recv()
    gp[...] = ((pre[...] + hr[...].astype(F32)) * slope[...]).astype(BF16)
    p_copy = remote(gp, gp_o, one_ss.at[3], one_rs.at[3], {"tok": tok_o})
    p_copy.start()
    p_copy.wait_recv()
    gp_both = jnp.concatenate([gp[...], gp_o[...]], axis=0)
    for i in range(half):
        dw = jnp.dot(xt[i], gp_both, preferred_element_type=F32)
        r = dw[main:main + rest]
        for g in range(1, groups):
            r = r + dw[main + g * rest:main + (g + 1) * rest]
        oe_ref[i * feats:(i + 1) * feats] = jnp.concatenate([dw[:main], r], axis=0).astype(BF16)

    x_done()
    g_done()
    for i in range(half):
        x_tok(i).wait_send()
    for j in range(n_lat):
        g_tok(j).wait_send()
    y_copy.wait_send()
    a_copy.wait_send()
    h_copy.wait_send()
    p_copy.wait_send()
    for c in range(CHUNKS):
        each(lambda d: x_send(z + d, c).wait_send())
        x_send(z, c).wait_send()
        each(lambda d: z_send(0 if d > 0 else 1, z + d, c).wait_send())


def fused_shards(n_lat, resid, w_enc, b_enc, w_dec, b_dec):
    x, we, wd = resid[0], w_enc[0], w_dec[0]
    rows, feats = x.shape
    total, hid = we.shape
    main = feats // LANES * LANES
    wide = main + LANES
    block = rows * feats // LANES
    half, nz = n_lat // 2, n_lat // 2
    dma = pltpu.SemaphoreType.DMA
    vm = pltpu.VMEM
    blocks = vm((n_lat, block, LANES), BF16)
    blocks_z = vm((nz, block, LANES), BF16)
    square = vm((rows, hid), BF16)
    in_vmem = pl.BlockSpec(memory_space=pltpu.VMEM)
    in_hbm = pl.BlockSpec(memory_space=pltpu.HBM)
    ge, gd = pl.pallas_call(
        functools.partial(kernel, n_lat, rows * 2),
        out_shape=(
            jax.ShapeDtypeStruct((half * feats, hid), BF16),
            jax.ShapeDtypeStruct((hid, total), BF16),
        ),
        in_specs=[in_hbm] * 5,
        out_specs=(in_vmem, in_vmem),
        scratch_shapes=[
            vm((rows, feats), BF16), vm((1, hid), F32), vm((1, feats), BF16),
            vm((total, hid), BF16),
            vm((hid, total), BF16),
            vm((n_lat, hid, wide), BF16),
            blocks,
            vm((half, block, LANES), BF16),
            vm((half, wide, 2 * rows), BF16),
            blocks, blocks,
            vm((rows, hid), F32), vm((rows, hid), F32),
            square, vm((hid, 2 * rows), BF16), square,
            square, square, square, square, square, square,
            blocks_z, blocks_z, blocks_z, vm((2, nz, block, LANES), BF16),
            vm((block, LANES), F32),
            dma((5,)),
            dma((4, n_lat, CHUNKS)), dma((n_lat, CHUNKS)), dma((half,)),
            dma((4, n_lat, CHUNKS)), dma((n_lat, CHUNKS)), dma((n_lat,)),
            dma((4,)), dma((4,)),
            dma((nz, CHUNKS)), dma((nz, CHUNKS)), dma((nz, CHUNKS)), dma((2, nz, CHUNKS)),
        ],
        compiler_params=pltpu.CompilerParams(
            collective_id=0, has_side_effects=True, vmem_limit_bytes=67043328
        ),
    )(x, we, b_enc.reshape(1, -1), wd, b_dec)
    return ge[None], gd[None]


def packs(mesh, rows, feats):
    rest = feats % LANES
    if mesh.shape["layer"] != 2 or mesh.shape["tok"] != 2 or mesh.shape["latent"] % 4:
        return False
    if rest == 0 or rest % 32 or LANES % rest:
        return False
    fits = rows % (16 * (LANES // rest)) == 0 and feats > LANES
    return fits and rows * feats // LANES % (16 * CHUNKS) == 0


def solution(mesh):
    def shards(resid, w_enc, b_enc, w_dec, b_dec):
        _, rows, feats = resid.shape
        if packs(mesh, rows, feats) and resid.shape[0] == 1:
            return fused_shards(mesh.shape["latent"], resid, w_enc, b_enc, w_dec, b_dec)
        return plain_shards(resid, w_enc, b_enc, w_dec, b_dec)

    placed = (
        P("layer", "tok", "latent"),
        P("layer", None, "latent"),
        P("latent"),
        P("layer", "latent", None),
        P("layer", "latent"),
    )
    return jax.shard_map(
        shards,
        mesh=mesh,
        in_specs=placed,
        out_specs=(P("layer", "tok", "latent"), P("layer", "latent", None)),
        check_vma=False,
    )
```
